32 devices in a mesh: groups: 2 (over y), rows: 4 (over z), cols: 4 (over x, core).
Axes of the slice: x: 2, y: 2, z: 4, core: 2. Of those that a mesh axis runs over, the one named last changes fastest.
Arguments:
- tokens: bfloat16 [128, 256, 512], P(('groups', 'rows'), 'cols'), parts along dimension 0, may hold values from -30 to 30
- qkv_weight: bfloat16 [512, 1536], replicated, may hold values from -0.25 to 0.25
- depth_kernel: float32 [25, 1536], replicated, may hold values from -1.25 to 1.25
- group_kernel: bfloat16 [48, 32, 32], replicated, may hold values from -1 to 1
- proj_weight: bfloat16 [1024, 512], replicated, may hold values from -0.1875 to 0.1875
- out_gain: float32 [512], replicated, may hold values from 4 to 16
- out_bias: float32 [512], replicated, may hold values from -3 to 3
Outputs:
- output: bfloat16 [128, 256, 512], P(('groups', 'rows'), 'cols'), parts along dimension 0
The draws below stay inside these ranges and needn't reach their ends.
There are 2 independent parts, one for each index of `groups`. The reference program is written for one: setup_inputs(seed, part) draws one part's arguments, and reference() takes and returns one part's arrays. A program takes and returns all parts, laid end to end along the dimension named above; an argument that names none is the same for every part. Nothing has to cross between parts.
All inputs are finite; a program needn't handle non-finite values.
Results may differ from the reference program's by a relative error of at most 0.0048.
Values may be sent and summed in bfloat16 or wider, within the bound.
A program may use at most 64 MiB of HBM per device.

```python
import math
import jax
import jax.numpy as jnp
from jax import lax

D = 512
HEAD_DIM = 32
HEADS = 16
TILE_ROWS = 16
HEIGHT = 64
WIDTH = 256
N_ROWS = 4


def draw_tokens(key, part):
    parts_keys = jax.random.split(key, 3)
    region_rows = HEIGHT // 4 + 1
    region_cols = WIDTH // 4 + 1
    region = jax.random.normal(parts_keys[0], (region_rows, region_cols, D), jnp.float32)
    region_scale = jnp.exp(jax.random.uniform(parts_keys[1], (region_rows, region_cols), jnp.float32, math.log(0.5), math.log(2.0)))
    row_of = jnp.arange(HEIGHT) // 4
    col_of = jnp.arange(WIDTH) // 4
    base = (region * region_scale[:, :, None])[row_of][:, col_of]
    rising = 1.0 + 2.0 * jnp.arange(HEIGHT, dtype=jnp.float32) / max(HEIGHT - 1, 1)
    noise = jax.random.normal(parts_keys[2], (HEIGHT, WIDTH, D), jnp.float32)
    field = 0.8 * base + 0.6 * noise
    return jnp.clip(field * rising[:, None, None], -30.0, 30.0).astype(jnp.bfloat16)


def bell_draw(key, dims, deviation, bound, kind=jnp.bfloat16):
    array = jax.random.normal(key, dims, jnp.float32) * deviation
    return jnp.minimum(jnp.maximum(array, -bound), bound).astype(kind)


def setup_inputs(seed: int = 0, part: int = 0) -> dict:
    keys = jax.random.split(jax.random.key(seed), 8)
    part_keys = jax.random.split(jax.random.fold_in(keys[7], part), 8)
    tokens = draw_tokens(jax.random.fold_in(jax.random.fold_in(keys[7], part), 71), part)
    qkv_weight = bell_draw(keys[1], (D, 3 * D), D ** -0.5, 0.25)
    depth_kernel = bell_draw(keys[2], (25, 3 * D), 25 ** -0.5, 1.25, jnp.float32)
    group_kernel = bell_draw(keys[3], (3 * HEADS, HEAD_DIM, HEAD_DIM), HEAD_DIM ** -0.5, 1.0)
    proj_weight = bell_draw(keys[4], (2 * D, D), (2 * D) ** -0.5, 0.1875)
    out_gain = jnp.clip(jnp.exp(jax.random.uniform(keys[5], (D,), jnp.float32, math.log(4.0), math.log(16.0))), 4.0, 16.0)
    out_bias = bell_draw(keys[6], (D,), 0.5, 3.0, jnp.float32)
    return dict(tokens=tokens, qkv_weight=qkv_weight, depth_kernel=depth_kernel, group_kernel=group_kernel, proj_weight=proj_weight, out_gain=out_gain, out_bias=out_bias)


def feature_map(inputs):
    return jax.nn.elu(inputs.astype(jnp.float32)) + 1.0


def aggregate(padded, depth_kernel, group_kernel, height, breadth):
    channels = padded.shape[2]
    summed = jnp.zeros((height, breadth, channels), jnp.float32)
    for offset_row in range(5):
        for offset_col in range(5):
            window = padded[offset_row:offset_row + height, offset_col:offset_col + breadth].astype(jnp.float32)
            summed = summed + window * depth_kernel[offset_row * 5 + offset_col]
    spread = summed.astype(jnp.bfloat16).reshape(height * breadth, channels // HEAD_DIM, HEAD_DIM)
    grouped = jnp.einsum("ngc,gcd->ngd", spread.astype(jnp.float32), group_kernel.astype(jnp.float32))
    return grouped.astype(jnp.bfloat16).reshape(height, breadth, channels)


def context_states(source):
    amount = source.shape[0]
    grouped = source.reshape(amount, -1, 3, HEAD_DIM)
    key_feats = feature_map(grouped[:, :, 1]).astype(jnp.bfloat16).astype(jnp.float32)
    values = grouped[:, :, 2].astype(jnp.float32)
    states = jnp.einsum("nhd,nhe->hde", key_feats, values)
    totals = jnp.sum(key_feats, axis=0)
    return states, totals


def reference(tokens, qkv_weight, depth_kernel, group_kernel, proj_weight, out_gain, out_bias):
    triple = jnp.dot(tokens.reshape(HEIGHT * WIDTH, D), qkv_weight, preferred_element_type=jnp.float32)
    triple = triple.astype(jnp.bfloat16).reshape(HEIGHT, WIDTH, 3 * D)
    padded = jnp.pad(triple, ((2, 2), (2, 2), (0, 0)))
    band_ids = jnp.arange(N_ROWS, dtype=jnp.int32)

    def band_aggregate(index):
        rows_in = lax.dynamic_slice_in_dim(padded, index * TILE_ROWS, TILE_ROWS + 4, 0)
        return aggregate(rows_in, depth_kernel, group_kernel, TILE_ROWS, WIDTH)

    aggregated = lax.map(band_aggregate, band_ids).reshape(HEIGHT, WIDTH, 3 * D)

    def band_pair(index):
        plain = lax.dynamic_slice_in_dim(triple, index * TILE_ROWS, TILE_ROWS, 0).reshape(-1, 3 * D)
        scaled = lax.dynamic_slice_in_dim(aggregated, index * TILE_ROWS, TILE_ROWS, 0).reshape(-1, 3 * D)
        return plain, scaled

    def band_states(index):
        plain, scaled = band_pair(index)
        plain_state, plain_total = context_states(plain)
        scaled_state, scaled_total = context_states(scaled)
        return jnp.concatenate([plain_state, scaled_state], 0), jnp.concatenate([plain_total, scaled_total], 0)

    band_s, band_z = lax.map(band_states, band_ids)
    states = jnp.sum(band_s, axis=0)
    totals = jnp.sum(band_z, axis=0)

    def band_output(index):
        plain, scaled = band_pair(index)
        amount = plain.shape[0]
        queries = jnp.concatenate([
            feature_map(plain.reshape(amount, -1, 3, HEAD_DIM)[:, :, 0]),
            feature_map(scaled.reshape(amount, -1, 3, HEAD_DIM)[:, :, 0])], 1)
        numerator = jnp.einsum("nhd,hde->nhe", queries, states, precision=lax.Precision.HIGHEST)
        denominator = jnp.einsum("nhd,hd->nh", queries, totals, precision=lax.Precision.HIGHEST)
        attended = (numerator / denominator[:, :, None]).astype(jnp.bfloat16).reshape(amount, 2 * D)
        projected = jnp.dot(attended, proj_weight, preferred_element_type=jnp.float32)
        source = lax.dynamic_slice_in_dim(tokens, index * TILE_ROWS, TILE_ROWS, 0).reshape(amount, D)
        result = source.astype(jnp.float32) + out_gain * projected + out_bias
        return result.astype(jnp.bfloat16)

    output = lax.map(band_output, band_ids)
    return output.reshape(HEIGHT, WIDTH, D)
```

```python
import functools

import jax
import jax.numpy as jnp
from jax import lax
from jax.experimental import pallas as pl
from jax.experimental.pallas import tpu as pltpu
from jax.sharding import PartitionSpec as P

HEAD_DIM = 32
PACK = 8 * HEAD_DIM
LANES = 128
SUB = 16
BF = jnp.bfloat16
F32 = jnp.float32
WAYS = ((1, 0), (-1, 0), (0, 1), (0, -1), (1, 1), (1, -1), (-1, 1), (-1, -1))


def iota(shape, dim):
    return lax.broadcasted_iota(jnp.int32, shape, dim)


def dot(a, b):
    return jnp.dot(a, b, preferred_element_type=F32)


def feature_map(u):
    return jnp.where(u > 0, u + 1.0, jnp.exp(jnp.minimum(u, 0.0)))


def one_hot(mask):
    return jnp.where(mask, 1.0, 0.0).astype(BF)


def kernel(
    n_rows, n_cols,
    tok_ref, w_ref, dk_ref, gk_ref, pw_ref, gain_ref, bias_ref,
    out_ref,
    stage_e, stage_c, halo_e, halo_c, halo_r, wq, taps, gbd, res, trip, spread, kfeat, acc,
    part, rs, ar_src, ar, ag,
    halo_send, halo_recv, red_send, red_recv,
):
    height, breadth, d = tok_ref.shape
    inner = breadth // SUB
    wide = inner + 4
    amount = height * breadth
    n_pack = d // PACK
    mr, mc = lax.axis_index("rows"), lax.axis_index("cols")

    def exists(way):
        r, c = mr + way[0], mc + way[1]
        return (r >= 0) & (r < n_rows) & (c >= 0) & (c < n_cols)

    def at(r, c):
        return {"rows": r, "cols": c}

    MESH = pl.DeviceIdType.MESH
    barrier = pltpu.get_barrier_semaphore()
    for k in range(1, n_rows):
        pl.semaphore_signal(barrier, inc=1, device_id=at(lax.rem(mr + k, n_rows), mc), device_id_type=MESH)
    for k in range(1, n_cols):
        pl.semaphore_signal(barrier, inc=1, device_id=at(mr, lax.rem(mc + k, n_cols)), device_id_type=MESH)
    for way in WAYS[4:]:
        @pl.when(exists(way))
        def _():
            pl.semaphore_signal(barrier, inc=1, device_id=at(mr + way[0], mc + way[1]), device_id_type=MESH)

    rows_out = 2 * 2 * height + 4 * SUB
    m = iota((rows_out, amount), 0)
    src = iota((rows_out, amount), 1)
    e = 2 * height
    right = (m >= e).astype(jnp.int32)
    me_ = m - right * e
    edge = (me_ // 2) * breadth + (me_ % 2) + right * (breadth - 2)
    cm = m - 2 * e
    ci, cr = cm // SUB, cm % SUB
    corner = ((cr // 2) + (ci // 2) * (height - 2)) * breadth + (cr % 2) + (ci % 2) * (breadth - 2)
    want = jnp.where(m < 2 * e, edge, jnp.where(cr < 4, corner, -1))
    sel = dot(one_hot(want == src), tok_ref[...].reshape(amount, d)).astype(BF)
    stage_e[...] = sel[: 2 * e].reshape(2, e, d)
    stage_c[...] = sel[2 * e :].reshape(4, SUB, d)

    moves = (
        (tok_ref.at[pl.ds(height - 2, 2)], halo_r.at[0]),
        (tok_ref.at[pl.ds(0, 2)], halo_r.at[1]),
        (stage_e.at[1], halo_e.at[0]),
        (stage_e.at[0], halo_e.at[1]),
        (stage_c.at[3], halo_c.at[0]),
        (stage_c.at[2], halo_c.at[1]),
        (stage_c.at[1], halo_c.at[2]),
        (stage_c.at[0], halo_c.at[3]),
    )

    def halo_copy(i):
        way = WAYS[i]
        return pltpu.make_async_remote_copy(
            src_ref=moves[i][0], dst_ref=moves[i][1],
            send_sem=halo_send.at[i], recv_sem=halo_recv.at[i],
            device_id=at(mr + way[0], mc + way[1]), device_id_type=MESH,
        )

    n_diag = sum(exists(way).astype(jnp.int32) for way in WAYS[4:])
    pl.semaphore_wait(barrier, n_rows - 1 + n_cols - 1 + n_diag)
    for i, way in enumerate(WAYS):
        @pl.when(exists(way))
        def _():
            halo_copy(i).start()

        @pl.when(jnp.logical_not(exists((-way[0], -way[1]))))
        def _():
            dst = moves[i][1]
            dst[...] = jnp.zeros(dst.shape, BF)

    third = 3 * PACK
    row, col = iota((third, third), 0), iota((third, third), 1)
    rem = col % PACK
    perm = one_hot(row == (rem // HEAD_DIM) * (3 * HEAD_DIM) + (col // PACK) * HEAD_DIM + rem % HEAD_DIM)
    for i in range(n_pack):
        wp = dot(w_ref[:, third * i : third * (i + 1)], perm).astype(BF)
        tp = dot(dk_ref[:, third * i : third * (i + 1)].astype(BF), perm)
        for t in range(3):
            lo = t * d + i * PACK
            wq[:, lo : lo + PACK] = wp[:, t * PACK : (t + 1) * PACK]
            for tap in range(25):
                taps[tap, :, lo : lo + PACK] = jnp.broadcast_to(
                    tp[tap : tap + 1, t * PACK : (t + 1) * PACK], (SUB, PACK)
                ).astype(BF)
    prow, pcol = iota((PACK, PACK), 0), iota((PACK, PACK), 1)
    same = prow // HEAD_DIM == pcol // HEAD_DIM
    tiled_eye = one_hot(iota((HEAD_DIM, PACK), 1) % HEAD_DIM == iota((HEAD_DIM, PACK), 0))
    for t in range(3):
        for i in range(n_pack):
            g = jnp.concatenate([gk_ref[3 * (8 * i + h) + t] for h in range(8)], axis=0)
            gbd[t * n_pack + i] = jnp.where(same, dot(g, tiled_eye), 0.0).astype(BF)

    for i, way in enumerate(WAYS):
        @pl.when(exists((-way[0], -way[1])))
        def _():
            halo_copy(i).wait_recv()

    halo = jnp.concatenate([halo_e[...].reshape(2 * e, d), halo_c[...].reshape(4 * SUB, d)], axis=0)
    base = 2 * breadth
    size_m, size_k = 2 * wide * SUB, base + 2 * e + 4 * SUB
    m, src = iota((size_m, size_k), 0), iota((size_m, size_k), 1)
    which = m // (wide * SUB)
    jj, s = (m // SUB) % wide, m % SUB
    c = inner * s + jj - 2
    for p in range(height // 2 + 2):
        if p == 0:
            pair, lo, hi, line = halo_r[0], base + 2 * e, base + 2 * e + SUB, 0
        elif p == height // 2 + 1:
            pair, lo, hi, line = halo_r[1], base + 2 * e + 2 * SUB, base + 2 * e + 3 * SUB, 0
        else:
            pair, lo, hi, line = tok_ref[2 * p - 2 : 2 * p], base, base + e, 2 * p - 2
        side = 2 * (which + line)
        want = jnp.where(c < 0, lo + side + c + 2, jnp.where(c >= breadth, hi + side + c - breadth, which * breadth + c))
        x = jnp.concatenate([pair.reshape(base, d), halo], axis=0)
        y = dot(one_hot(want == src), x).astype(BF)
        if 0 < p < height // 2 + 1:
            res[2 * p - 2 : 2 * p] = y.reshape(2, wide, SUB, d)[:, 2 : 2 + inner]
        trip[2 * p : 2 * p + 2] = dot(y, wq[...]).astype(BF).reshape(2, wide, SUB, 3 * d)

    zrow, zcol = iota((PACK, LANES), 0), iota((PACK, LANES), 1)
    ones = jnp.ones((amount, LANES), BF)
    dn = (((0,), (0,)), ((), ()))

    def local_states(z, get_k, get_v):
        total = jnp.zeros((HEAD_DIM, LANES), F32)
        pieces = []
        for i in range(n_pack):
            k, v = get_k(i), get_v(i)
            st = lax.dot_general(k, v, dn, preferred_element_type=F32)
            pieces.append(jnp.sum(jnp.where(same, st, 0.0).reshape(8, HEAD_DIM, PACK), axis=0))
            tot = lax.dot_general(k, ones, dn, preferred_element_type=F32)
            tot = jnp.where(zcol == 8 * i + zrow // HEAD_DIM, tot, 0.0)
            total = total + jnp.sum(tot.reshape(8, HEAD_DIM, LANES), axis=0)
        flat = jnp.concatenate(pieces + [total], axis=1)
        step = HEAD_DIM // n_cols
        for q in range(n_cols):
            part[z, q] = flat[q * step : (q + 1) * step]

    def rs_copy(z, k):
        peer = lax.rem(mc + k, n_cols)
        return pltpu.make_async_remote_copy(
            src_ref=part.at[z, peer], dst_ref=rs.at[z, k - 1],
            send_sem=red_send.at[z, 0, k - 1], recv_sem=red_recv.at[z, 0, k - 1],
            device_id=at(mr, peer), device_id_type=MESH,
        )

    def ar_copy(z, k):
        return pltpu.make_async_remote_copy(
            src_ref=ar_src.at[z], dst_ref=ar.at[z, k - 1],
            send_sem=red_send.at[z, 1, k - 1], recv_sem=red_recv.at[z, 1, k - 1],
            device_id=at(lax.rem(mr + k, n_rows), mc), device_id_type=MESH,
        )

    def ag_copy(z, k):
        return pltpu.make_async_remote_copy(
            src_ref=ag.at[z, mc], dst_ref=ag.at[z, mc],
            send_sem=red_send.at[z, 2, k - 1], recv_sem=red_recv.at[z, 2, k - 1],
            device_id=at(mr, lax.rem(mc + k, n_cols)), device_id_type=MESH,
        )

    def ag_wait(z, k):
        sender = lax.rem(mc - k + n_cols, n_cols)
        pltpu.make_async_remote_copy(
            src_ref=ag.at[z, mc], dst_ref=ag.at[z, sender],
            send_sem=red_send.at[z, 2, k - 1], recv_sem=red_recv.at[z, 2, k - 1],
            device_id=at(mr, sender), device_id_type=MESH,
        ).wait_recv()

    def reduce_1(z):
        for k in range(1, n_cols):
            rs_copy(z, k).start()

    def reduce_2(z):
        total = part[z, mc]
        for k in range(1, n_cols):
            rs_copy(z, k).wait_recv()
            total = total + rs[z, k - 1]
        ar_src[z] = total
        for k in range(1, n_rows):
            ar_copy(z, k).start()

    def reduce_3(z):
        total = ar_src[z]
        for k in range(1, n_rows):
            ar_copy(z, k).wait_recv()
            total = total + ar[z, k - 1]
        ag[z, mc] = total
        for k in range(1, n_cols):
            ag_copy(z, k).start()

    def reduce_4(z):
        for k in range(1, n_cols):
            ag_wait(z, k)
        return jnp.concatenate([ag[z, q] for q in range(n_cols)], axis=0)

    def conv(first, last):
        def chunk(ch, _):
            lanes = pl.ds(pl.multiple_of(ch * LANES, LANES), LANES)
            w = [taps[t, :, lanes] for t in range(25)]

            def line(r, _):
                sums = [None] * inner
                for a in range(5):
                    xs = [trip[r + a, jj, :, lanes] for jj in range(wide)]
                    for j in range(inner):
                        term = xs[j] * w[5 * a]
                        for b in range(1, 5):
                            term = term + xs[j + b] * w[5 * a + b]
                        sums[j] = term if a == 0 else sums[j] + term
                for j in range(inner):
                    spread[r, j, :, lanes] = sums[j]
                return 0

            lax.fori_loop(0, height, line, 0)
            return 0

        lax.fori_loop(first, last, chunk, 0)

    def native(t, i):
        lo = t * d + i * PACK
        return trip[2 : 2 + height, 2 : 2 + inner, :, lo : lo + PACK].reshape(amount, PACK)

    def grouped(t, i):
        lo = t * d + i * PACK
        return dot(spread[:, :, :, lo : lo + PACK].reshape(amount, PACK), gbd[t * n_pack + i]).astype(BF)

    def attend(z, flat, get_q):
        for i in range(n_pack):
            st = flat[:, i * PACK : (i + 1) * PACK]
            st = jnp.where(same, jnp.concatenate([st] * 8, axis=0), 0.0).astype(BF)
            head = one_hot(iota((LANES, PACK), 0) == 8 * i + iota((LANES, PACK), 1) // HEAD_DIM)
            tot = dot(flat[:, n_pack * PACK :].astype(BF), head)
            tot = jnp.where(same, jnp.concatenate([tot] * 8, axis=0), 0.0).astype(BF)
            q = feature_map(get_q(i).astype(F32)).astype(BF)
            att = (dot(q, st) / dot(q, tot)).astype(BF)
            add = dot(att, pw_ref[z * d + i * PACK : z * d + (i + 1) * PACK, :])
            if z == 0 and i == 0:
                acc[...] = add
            else:
                acc[...] += add

    n_chunk = d // LANES
    local_states(0, lambda i: feature_map(native(1, i).astype(F32)).astype(BF), lambda i: native(2, i))
    reduce_1(0)
    conv(n_chunk, 2 * n_chunk)
    reduce_2(0)
    conv(2 * n_chunk, 3 * n_chunk)
    reduce_3(0)
    local_states(1, lambda i: feature_map(grouped(1, i).astype(F32)).astype(BF), lambda i: grouped(2, i))
    reduce_1(1)
    conv(0, n_chunk)
    reduce_2(1)
    attend(0, reduce_4(0), lambda i: native(0, i))
    reduce_3(1)
    attend(1, reduce_4(1), lambda i: grouped(0, i))

    lines = 4
    size = lines * breadth
    m, src = iota((size, size), 0), iota((size, size), 1)
    cc = m % breadth
    back = one_hot(src == (m // breadth) * breadth + (cc % inner) * SUB + cc // inner)
    for b in range(height // lines):
        got = acc[b * size : (b + 1) * size, :] * gain_ref[...] + bias_ref[...]
        got = (got + res[b * lines : (b + 1) * lines].reshape(size, d).astype(F32)).astype(BF)
        out_ref[b * lines : (b + 1) * lines] = dot(back, got).astype(BF).reshape(lines, breadth, d)

    for i, way in enumerate(WAYS):
        @pl.when(exists(way))
        def _():
            halo_copy(i).wait_send()
    for z in range(2):
        for k in range(1, n_cols):
            rs_copy(z, k).wait_send()
            ag_copy(z, k).wait_send()
        for k in range(1, n_rows):
            ar_copy(z, k).wait_send()


def body(n_rows, n_cols, tokens, qkv_weight, depth_kernel, group_kernel, proj_weight, out_gain, out_bias):
    height, breadth, d = tokens.shape
    inner = breadth // SUB
    step = HEAD_DIM // n_cols
    msg = d + LANES
    most = max(n_rows, n_cols)
    vmem = pl.BlockSpec(memory_space=pltpu.VMEM)
    return pl.pallas_call(
        functools.partial(kernel, n_rows, n_cols),
        out_shape=jax.ShapeDtypeStruct((height, breadth, d), BF),
        in_specs=[vmem] * 7,
        out_specs=vmem,
        scratch_shapes=[
            pltpu.VMEM((2, 2 * height, d), BF),
            pltpu.VMEM((4, SUB, d), BF),
            pltpu.VMEM((2, 2 * height, d), BF),
            pltpu.VMEM((4, SUB, d), BF),
            pltpu.VMEM((2, 2, breadth, d), BF),
            pltpu.VMEM((d, 3 * d), BF),
            pltpu.VMEM((25, SUB, 3 * d), BF),
            pltpu.VMEM((3 * d // PACK, PACK, PACK), BF),
            pltpu.VMEM((height, inner, SUB, d), BF),
            pltpu.VMEM((height + 4, inner + 4, SUB, 3 * d), BF),
            pltpu.VMEM((height, inner, SUB, 3 * d), BF),
            pltpu.VMEM((8, LANES), BF),
            pltpu.VMEM((height * breadth, d), F32),
            pltpu.VMEM((2, n_cols, step, msg), F32),
            pltpu.VMEM((2, n_cols - 1, step, msg), F32),
            pltpu.VMEM((2, step, msg), F32),
            pltpu.VMEM((2, n_rows - 1, step, msg), F32),
            pltpu.VMEM((2, n_cols, step, msg), F32),
            pltpu.SemaphoreType.DMA((8,)),
            pltpu.SemaphoreType.DMA((8,)),
            pltpu.SemaphoreType.DMA((2, 3, most)),
            pltpu.SemaphoreType.DMA((2, 3, most)),
        ],
        compiler_params=pltpu.CompilerParams(
            collective_id=0, has_side_effects=True, vmem_limit_bytes=56 * 1024 * 1024
        ),
        name="attention_module",
    )(tokens, qkv_weight, depth_kernel, group_kernel, proj_weight, out_gain[None, :], out_bias[None, :])


def solution(mesh):
    placed = (P(("groups", "rows"), "cols", None), P(), P(), P(), P(), P(), P())
    return jax.shard_map(
        functools.partial(body, mesh.shape["rows"], mesh.shape["cols"]),
        mesh=mesh,
        in_specs=placed,
        out_specs=P(("groups", "rows"), "cols", None),
        check_vma=False,
    )
```

```python
import functools

import jax
import jax.numpy as jnp
from jax import lax
from jax.experimental import pallas as pl
from jax.experimental.pallas import tpu as pltpu
from jax.sharding import PartitionSpec as P

HEAD_DIM = 32
PACK = 8 * HEAD_DIM
LANES = 128
SUB = 16
BF = jnp.bfloat16
F32 = jnp.float32
WAYS = ((1, 0), (-1, 0), (0, 1), (0, -1), (1, 1), (1, -1), (-1, 1), (-1, -1))


def iota(shape, dim):
    return lax.broadcasted_iota(jnp.int32, shape, dim)


def dot(a, b):
    return jnp.dot(a, b, preferred_element_type=F32)


def feature_map(u):
    return jnp.where(u > 0, u + 1.0, jnp.exp(jnp.minimum(u, 0.0)))


def one_hot(mask):
    return jnp.where(mask, 1.0, 0.0).astype(BF)


def kernel(
    n_rows, n_cols,
    tok_ref, w_ref, dk_ref, gk_ref, pw_ref, gain_ref, bias_ref,
    out_ref,
    stage_e, stage_c, halo_e, halo_c, halo_r, wq, taps, gbd, res, trip, spread, acc,
    part, rs, ar_src, ar, ag,
    halo_send, halo_recv, red_send, red_recv,
):
    height, breadth, d = tok_ref.shape
    inner = breadth // SUB
    wide = inner + 4
    amount = height * breadth
    n_pack = d // PACK
    mr, mc = lax.axis_index("rows"), lax.axis_index("cols")

    def exists(way):
        r, c = mr + way[0], mc + way[1]
        return (r >= 0) & (r < n_rows) & (c >= 0) & (c < n_cols)

    def at(r, c):
        return {"rows": r, "cols": c}

    MESH = pl.DeviceIdType.MESH
    barrier = pltpu.get_barrier_semaphore()
    for k in range(1, n_rows):
        pl.semaphore_signal(barrier, inc=1, device_id=at(lax.rem(mr + k, n_rows), mc), device_id_type=MESH)
    for k in range(1, n_cols):
        pl.semaphore_signal(barrier, inc=1, device_id=at(mr, lax.rem(mc + k, n_cols)), device_id_type=MESH)
    for way in WAYS[4:]:
        @pl.when(exists(way))
        def _():
            pl.semaphore_signal(barrier, inc=1, device_id=at(mr + way[0], mc + way[1]), device_id_type=MESH)

    rows_out = 2 * 2 * height + 4 * SUB
    m = iota((rows_out, amount), 0)
    src = iota((rows_out, amount), 1)
    e = 2 * height
    right = (m >= e).astype(jnp.int32)
    me_ = m - right * e
    edge = (me_ // 2) * breadth + (me_ % 2) + right * (breadth - 2)
    cm = m - 2 * e
    ci, cr = cm // SUB, cm % SUB
    corner = ((cr // 2) + (ci // 2) * (height - 2)) * breadth + (cr % 2) + (ci % 2) * (breadth - 2)
    want = jnp.where(m < 2 * e, edge, jnp.where(cr < 4, corner, -1))
    sel = dot(one_hot(want == src), tok_ref[...].reshape(amount, d)).astype(BF)
    stage_e[...] = sel[: 2 * e].reshape(2, e, d)
    stage_c[...] = sel[2 * e :].reshape(4, SUB, d)

    moves = (
        (tok_ref.at[pl.ds(height - 2, 2)], halo_r.at[0]),
        (tok_ref.at[pl.ds(0, 2)], halo_r.at[1]),
        (stage_e.at[1], halo_e.at[0]),
        (stage_e.at[0], halo_e.at[1]),
        (stage_c.at[3], halo_c.at[0]),
        (stage_c.at[2], halo_c.at[1]),
        (stage_c.at[1], halo_c.at[2]),
        (stage_c.at[0], halo_c.at[3]),
    )

    def halo_copy(i):
        way = WAYS[i]
        return pltpu.make_async_remote_copy(
            src_ref=moves[i][0], dst_ref=moves[i][1],
            send_sem=halo_send.at[i], recv_sem=halo_recv.at[i],
            device_id=at(mr + way[0], mc + way[1]), device_id_type=MESH,
        )

    third = 3 * PACK
    row, col = iota((third, third), 0), iota((third, third), 1)
    rem = col % PACK
    perm = one_hot(row == (rem // HEAD_DIM) * (3 * HEAD_DIM) + (col // PACK) * HEAD_DIM + rem % HEAD_DIM)
    for i in range(n_pack):
        wp = dot(w_ref[:, third * i : third * (i + 1)], perm).astype(BF)
        for t in range(3):
            lo = t * d + i * PACK
            wq[:, lo : lo + PACK] = wp[:, t * PACK : (t + 1) * PACK]
    prow, pcol = iota((PACK, PACK), 0), iota((PACK, PACK), 1)
    same = prow // HEAD_DIM == pcol // HEAD_DIM
    base = 2 * breadth
    size_m = 2 * wide * SUB
    m, src = iota((size_m, base), 0), iota((size_m, base), 1)
    which = m // (wide * SUB)
    c = inner * (m % SUB) + (m // SUB) % wide - 2
    inside = (c >= 0) & (c < breadth)
    place = one_hot((which * breadth + c == src) & inside)
    for p in range(height // 2):
        y = dot(place, tok_ref[2 * p : 2 * p + 2].reshape(base, d)).astype(BF)
        res[2 * p : 2 * p + 2] = y.reshape(2, wide, SUB, d)[:, 2 : 2 + inner]
        trip[2 * p + 2 : 2 * p + 4] = dot(y, wq[...]).astype(BF).reshape(2, wide, SUB, 3 * d)

    n_diag = sum(exists(way).astype(jnp.int32) for way in WAYS[4:])
    pl.semaphore_wait(barrier, n_rows - 1 + n_cols - 1 + n_diag)
    for i, way in enumerate(WAYS):
        @pl.when(exists(way))
        def _():
            halo_copy(i).start()

        @pl.when(jnp.logical_not(exists((-way[0], -way[1]))))
        def _():
            dst = moves[i][1]
            dst[...] = jnp.zeros(dst.shape, BF)

    zrow, zcol = iota((PACK, LANES), 0), iota((PACK, LANES), 1)
    ones = jnp.ones((amount, LANES), BF)
    dn = (((0,), (0,)), ((), ()))

    def local_states(z, get_k, get_v):
        total = jnp.zeros((HEAD_DIM, LANES), F32)
        pieces = []
        for i in range(n_pack):
            k, v = get_k(i), get_v(i)
            st = lax.dot_general(k, v, dn, preferred_element_type=F32)
            pieces.append(jnp.sum(jnp.where(same, st, 0.0).reshape(8, HEAD_DIM, PACK), axis=0))
            tot = lax.dot_general(k, ones, dn, preferred_element_type=F32)
            tot = jnp.where(zcol == 8 * i + zrow // HEAD_DIM, tot, 0.0)
            total = total + jnp.sum(tot.reshape(8, HEAD_DIM, LANES), axis=0)
        flat = jnp.concatenate(pieces + [total], axis=1)
        step = HEAD_DIM // n_cols
        for q in range(n_cols):
            part[z, q] = flat[q * step : (q + 1) * step]

    def rs_copy(z, k):
        peer = lax.rem(mc + k, n_cols)
        return pltpu.make_async_remote_copy(
            src_ref=part.at[z, peer], dst_ref=rs.at[z, k - 1],
            send_sem=red_send.at[z, 0, k - 1], recv_sem=red_recv.at[z, 0, k - 1],
            device_id=at(mr, peer), device_id_type=MESH,
        )

    def ar_copy(z, k):
        return pltpu.make_async_remote_copy(
            src_ref=ar_src.at[z], dst_ref=ar.at[z, k - 1],
            send_sem=red_send.at[z, 1, k - 1], recv_sem=red_recv.at[z, 1, k - 1],
            device_id=at(lax.rem(mr + k, n_rows), mc), device_id_type=MESH,
        )

    def ag_copy(z, k):
        return pltpu.make_async_remote_copy(
            src_ref=ag.at[z, mc], dst_ref=ag.at[z, mc],
            send_sem=red_send.at[z, 2, k - 1], recv_sem=red_recv.at[z, 2, k - 1],
            device_id=at(mr, lax.rem(mc + k, n_cols)), device_id_type=MESH,
        )

    def ag_wait(z, k):
        sender = lax.rem(mc - k + n_cols, n_cols)
        pltpu.make_async_remote_copy(
            src_ref=ag.at[z, mc], dst_ref=ag.at[z, sender],
            send_sem=red_send.at[z, 2, k - 1], recv_sem=red_recv.at[z, 2, k - 1],
            device_id=at(mr, sender), device_id_type=MESH,
        ).wait_recv()

    def reduce_1(z):
        for k in range(1, n_cols):
            rs_copy(z, k).start()

    def reduce_2(z):
        total = part[z, mc]
        for k in range(1, n_cols):
            rs_copy(z, k).wait_recv()
            total = total + rs[z, k - 1]
        ar_src[z] = total
        for k in range(1, n_rows):
            ar_copy(z, k).start()

    def reduce_3(z):
        total = ar_src[z]
        for k in range(1, n_rows):
            ar_copy(z, k).wait_recv()
            total = total + ar[z, k - 1]
        ag[z, mc] = total
        for k in range(1, n_cols):
            ag_copy(z, k).start()

    def reduce_4(z):
        for k in range(1, n_cols):
            ag_wait(z, k)
        return jnp.concatenate([ag[z, q] for q in range(n_cols)], axis=0)

    def conv(first, last):
        def chunk(ch, _):
            lanes = pl.ds(pl.multiple_of(ch * LANES, LANES), LANES)
            w = [taps[t, :, lanes] for t in range(25)]

            def line(r, _):
                sums = [None] * inner
                for a in range(5):
                    xs = [trip[r + a, jj, :, lanes] for jj in range(wide)]
                    for j in range(inner):
                        term = xs[j] * w[5 * a]
                        for b in range(1, 5):
                            term = term + xs[j + b] * w[5 * a + b]
                        sums[j] = term if a == 0 else sums[j] + term
                for j in range(inner):
                    spread[r, j, :, lanes] = sums[j]
                return 0

            lax.fori_loop(0, height, line, 0)
            return 0

        lax.fori_loop(first, last, chunk, 0)

    def native(t, i):
        lo = t * d + i * PACK
        return trip[2 : 2 + height, 2 : 2 + inner, :, lo : lo + PACK].reshape(amount, PACK)

    def grouped(t, i):
        lo = t * d + i * PACK
        return dot(spread[:, :, :, lo : lo + PACK].reshape(amount, PACK), gbd[t * n_pack + i]).astype(BF)

    def attend(z, flat, get_q):
        for i in range(n_pack):
            st = flat[:, i * PACK : (i + 1) * PACK]
            st = jnp.where(same, jnp.concatenate([st] * 8, axis=0), 0.0).astype(BF)
            head = one_hot(iota((LANES, PACK), 0) == 8 * i + iota((LANES, PACK), 1) // HEAD_DIM)
            tot = dot(flat[:, n_pack * PACK :].astype(BF), head)
            tot = jnp.where(same, jnp.concatenate([tot] * 8, axis=0), 0.0).astype(BF)
            q = feature_map(get_q(i).astype(F32)).astype(BF)
            att = (dot(q, st) / dot(q, tot)).astype(BF)
            add = dot(att, pw_ref[z * d + i * PACK : z * d + (i + 1) * PACK, :])
            if z == 0 and i == 0:
                acc[...] = add
            else:
                acc[...] += add

    local_states(0, lambda i: feature_map(native(1, i).astype(F32)).astype(BF), lambda i: native(2, i))
    reduce_1(0)
    for i in range(n_pack):
        tp = dot(dk_ref[:, third * i : third * (i + 1)].astype(BF), perm)
        for t in range(3):
            lo = t * d + i * PACK
            for tap in range(25):
                taps[tap, :, lo : lo + PACK] = jnp.broadcast_to(
                    tp[tap : tap + 1, t * PACK : (t + 1) * PACK], (SUB, PACK)
                ).astype(BF)
    n_group = gk_ref.shape[2]
    gk = gk_ref[...].reshape(HEAD_DIM * HEAD_DIM, n_group)
    grow, gcol = iota((n_group, PACK), 0), iota((n_group, PACK), 1)
    keep = iota((HEAD_DIM * HEAD_DIM, PACK), 0) % HEAD_DIM == iota((HEAD_DIM * HEAD_DIM, PACK), 1) % HEAD_DIM
    for t in range(3):
        for i in range(n_pack):
            g = dot(gk, one_hot(grow == 3 * (8 * i + gcol // HEAD_DIM) + t))
            g = jnp.sum(jnp.where(keep, g, 0.0).reshape(HEAD_DIM, HEAD_DIM, PACK), axis=1)
            gbd[t * n_pack + i] = jnp.where(same, jnp.concatenate([g] * 8, axis=0), 0.0).astype(BF)

    for i, way in enumerate(WAYS):
        @pl.when(exists((-way[0], -way[1])))
        def _():
            halo_copy(i).wait_recv()


    corners = halo_c[...].reshape(4 * SUB, d)
    size_k = base + 4 * SUB
    m, src = iota((size_m, size_k), 0), iota((size_m, size_k), 1)
    which = m // (wide * SUB)
    c = inner * (m % SUB) + (m // SUB) % wide - 2
    for p in range(2):
        lo = base + 2 * p * SUB + 2 * which
        want = jnp.where(c < 0, lo + c + 2, jnp.where(c >= breadth, lo + SUB + c - breadth, which * breadth + c))
        y = dot(one_hot(want == src), jnp.concatenate([halo_r[p].reshape(base, d), corners], axis=0)).astype(BF)
        first = p * (height + 2)
        trip[first : first + 2] = dot(y, wq[...]).astype(BF).reshape(2, wide, SUB, 3 * d)
    sides = dot(halo_e[...].reshape(2 * e, d), wq[...])
    spot = iota((SUB, 3 * d), 0)
    masks = (one_hot(spot == 0), one_hot(spot == SUB - 1))
    for r in range(height):
        for side in range(2):
            for b in range(2):
                at_row = side * e + 2 * r + b
                jj = side * (inner + 2) + b
                line = jnp.broadcast_to(sides[at_row : at_row + 1], (SUB, 3 * d)).astype(BF)
                trip[r + 2, jj] = trip[r + 2, jj] + line * masks[side]

    n_chunk = d // LANES
    conv(n_chunk, 2 * n_chunk)
    reduce_2(0)
    conv(2 * n_chunk, 3 * n_chunk)
    reduce_3(0)
    local_states(1, lambda i: feature_map(grouped(1, i).astype(F32)).astype(BF), lambda i: grouped(2, i))
    reduce_1(1)
    conv(0, n_chunk)
    reduce_2(1)
    attend(0, reduce_4(0), lambda i: native(0, i))
    reduce_3(1)
    attend(1, reduce_4(1), lambda i: grouped(0, i))

    lines = 4
    size = lines * breadth
    m, src = iota((size, size), 0), iota((size, size), 1)
    cc = m % breadth
    back = one_hot(src == (m // breadth) * breadth + (cc % inner) * SUB + cc // inner)
    for b in range(height // lines):
        got = acc[b * size : (b + 1) * size, :] * gain_ref[...] + bias_ref[...]
        got = (got + res[b * lines : (b + 1) * lines].reshape(size, d).astype(F32)).astype(BF)
        out_ref[b * lines : (b + 1) * lines] = dot(back, got).astype(BF).reshape(lines, breadth, d)

    for i, way in enumerate(WAYS):
        @pl.when(exists(way))
        def _():
            halo_copy(i).wait_send()
    for z in range(2):
        for k in range(1, n_cols):
            rs_copy(z, k).wait_send()
            ag_copy(z, k).wait_send()
        for k in range(1, n_rows):
            ar_copy(z, k).wait_send()


def body(n_rows, n_cols, tokens, qkv_weight, depth_kernel, group_kernel, proj_weight, out_gain, out_bias):
    height, breadth, d = tokens.shape
    inner = breadth // SUB
    step = HEAD_DIM // n_cols
    msg = d + LANES
    most = max(n_rows, n_cols)
    vmem = pl.BlockSpec(memory_space=pltpu.VMEM)
    return pl.pallas_call(
        functools.partial(kernel, n_rows, n_cols),
        out_shape=jax.ShapeDtypeStruct((height, breadth, d), BF),
        in_specs=[vmem] * 7,
        out_specs=vmem,
        scratch_shapes=[
            pltpu.VMEM((2, 2 * height, d), BF),
            pltpu.VMEM((4, SUB, d), BF),
            pltpu.VMEM((2, 2 * height, d), BF),
            pltpu.VMEM((4, SUB, d), BF),
            pltpu.VMEM((2, 2, breadth, d), BF),
            pltpu.VMEM((d, 3 * d), BF),
            pltpu.VMEM((25, SUB, 3 * d), BF),
            pltpu.VMEM((3 * d // PACK, PACK, PACK), BF),
            pltpu.VMEM((height, inner, SUB, d), BF),
            pltpu.VMEM((height + 4, inner + 4, SUB, 3 * d), BF),
            pltpu.VMEM((height, inner, SUB, 3 * d), BF),
            pltpu.VMEM((height * breadth, d), F32),
            pltpu.VMEM((2, n_cols, step, msg), F32),
            pltpu.VMEM((2, n_cols - 1, step, msg), F32),
            pltpu.VMEM((2, step, msg), F32),
            pltpu.VMEM((2, n_rows - 1, step, msg), F32),
            pltpu.VMEM((2, n_cols, step, msg), F32),
            pltpu.SemaphoreType.DMA((8,)),
            pltpu.SemaphoreType.DMA((8,)),
            pltpu.SemaphoreType.DMA((2, 3, most)),
            pltpu.SemaphoreType.DMA((2, 3, most)),
        ],
        compiler_params=pltpu.CompilerParams(
            collective_id=0, has_side_effects=True, vmem_limit_bytes=56 * 1024 * 1024
        ),
        name="attention_module",
    )(tokens, qkv_weight, depth_kernel, jnp.transpose(group_kernel, (1, 2, 0)), proj_weight, out_gain[None, :], out_bias[None, :])


def solution(mesh):
    placed = (P(("groups", "rows"), "cols", None), P(), P(), P(), P(), P(), P())
    return jax.shard_map(
        functools.partial(body, mesh.shape["rows"], mesh.shape["cols"]),
        mesh=mesh,
        in_specs=placed,
        out_specs=P(("groups", "rows"), "cols", None),
        check_vma=False,
    )
```

```python
import functools

import jax
import jax.numpy as jnp
from jax import lax
from jax.experimental import pallas as pl
from jax.experimental.pallas import tpu as pltpu
from jax.sharding import PartitionSpec as P

HEAD_DIM = 32
PACK = 8 * HEAD_DIM
LANES = 128
SUB = 16
BF = jnp.bfloat16
F32 = jnp.float32
WAYS = ((1, 0), (-1, 0), (0, 1), (0, -1), (1, 1), (1, -1), (-1, 1), (-1, -1))


def iota(shape, dim):
    return lax.broadcasted_iota(jnp.int32, shape, dim)


def dot(a, b):
    return jnp.dot(a, b, preferred_element_type=F32)


def feature_map(u):
    return jnp.where(u > 0, u + 1.0, jnp.exp(jnp.minimum(u, 0.0)))


def one_hot(mask):
    return jnp.where(mask, 1.0, 0.0).astype(BF)


def kernel(
    n_rows, n_cols,
    tok_ref, w_ref, dk_ref, gk_ref, pw_ref, gain_ref, bias_ref,
    out_ref,
    stage_e, stage_c, halo_e, halo_c, halo_r, wq, taps, gbd, res, trip, spread, acc,
    part, rs, ar_src, ar, ag,
    halo_send, halo_recv, red_send, red_recv,
):
    height, breadth, d = tok_ref.shape
    inner = breadth // SUB
    wide = inner + 4
    amount = height * breadth
    n_pack = d // PACK
    mr, mc = lax.axis_index("rows"), lax.axis_index("cols")

    def exists(way):
        r, c = mr + way[0], mc + way[1]
        return (r >= 0) & (r < n_rows) & (c >= 0) & (c < n_cols)

    def at(r, c):
        return {"rows": r, "cols": c}

    MESH = pl.DeviceIdType.MESH
    barrier = pltpu.get_barrier_semaphore()
    for k in range(1, n_rows):
        pl.semaphore_signal(barrier, inc=1, device_id=at(lax.rem(mr + k, n_rows), mc), device_id_type=MESH)
    for k in range(1, n_cols):
        pl.semaphore_signal(barrier, inc=1, device_id=at(mr, lax.rem(mc + k, n_cols)), device_id_type=MESH)
    for way in WAYS[4:]:
        @pl.when(exists(way))
        def _():
            pl.semaphore_signal(barrier, inc=1, device_id=at(mr + way[0], mc + way[1]), device_id_type=MESH)

    rows_out = 2 * 2 * height + 4 * SUB
    m = iota((rows_out, amount), 0)
    src = iota((rows_out, amount), 1)
    e = 2 * height
    right = (m >= e).astype(jnp.int32)
    me_ = m - right * e
    edge = (me_ // 2) * breadth + (me_ % 2) + right * (breadth - 2)
    cm = m - 2 * e
    ci, cr = cm // SUB, cm % SUB
    corner = ((cr // 2) + (ci // 2) * (height - 2)) * breadth + (cr % 2) + (ci % 2) * (breadth - 2)
    want = jnp.where(m < 2 * e, edge, jnp.where(cr < 4, corner, -1))
    sel = dot(one_hot(want == src), tok_ref[...].reshape(amount, d)).astype(BF)
    stage_e[...] = sel[: 2 * e].reshape(2, e, d)
    stage_c[...] = sel[2 * e :].reshape(4, SUB, d)

    moves = (
        (tok_ref.at[pl.ds(height - 2, 2)], halo_r.at[0]),
        (tok_ref.at[pl.ds(0, 2)], halo_r.at[1]),
        (stage_e.at[1], halo_e.at[0]),
        (stage_e.at[0], halo_e.at[1]),
        (stage_c.at[3], halo_c.at[0]),
        (stage_c.at[2], halo_c.at[1]),
        (stage_c.at[1], halo_c.at[2]),
        (stage_c.at[0], halo_c.at[3]),
    )

    def halo_copy(i):
        way = WAYS[i]
        return pltpu.make_async_remote_copy(
            src_ref=moves[i][0], dst_ref=moves[i][1],
            send_sem=halo_send.at[i], recv_sem=halo_recv.at[i],
            device_id=at(mr + way[0], mc + way[1]), device_id_type=MESH,
        )

    third = 3 * PACK
    row, col = iota((third, third), 0), iota((third, third), 1)
    rem = col % PACK
    perm = one_hot(row == (rem // HEAD_DIM) * (3 * HEAD_DIM) + (col // PACK) * HEAD_DIM + rem % HEAD_DIM)
    for i in range(n_pack):
        wp = dot(w_ref[:, third * i : third * (i + 1)], perm).astype(BF)
        for t in range(3):
            lo = t * d + i * PACK
            wq[:, lo : lo + PACK] = wp[:, t * PACK : (t + 1) * PACK]
    prow, pcol = iota((PACK, PACK), 0), iota((PACK, PACK), 1)
    same = prow // HEAD_DIM == pcol // HEAD_DIM
    base = 2 * breadth
    size_m = 2 * wide * SUB
    m, src = iota((size_m, base), 0), iota((size_m, base), 1)
    which = m // (wide * SUB)
    c = inner * (m % SUB) + (m // SUB) % wide - 2
    inside = (c >= 0) & (c < breadth)
    place = one_hot((which * breadth + c == src) & inside)
    for p in range(height // 2):
        y = dot(place, tok_ref[2 * p : 2 * p + 2].reshape(base, d)).astype(BF)
        res[2 * p : 2 * p + 2] = y.reshape(2, wide, SUB, d)[:, 2 : 2 + inner]
        trip[2 * p + 2 : 2 * p + 4] = dot(y, wq[...]).astype(BF).reshape(2, wide, SUB, 3 * d)

    n_diag = sum(exists(way).astype(jnp.int32) for way in WAYS[4:])
    pl.semaphore_wait(barrier, n_rows - 1 + n_cols - 1 + n_diag)
    for i, way in enumerate(WAYS):
        @pl.when(exists(way))
        def _():
            halo_copy(i).start()

        @pl.when(jnp.logical_not(exists((-way[0], -way[1]))))
        def _():
            dst = moves[i][1]
            dst[...] = jnp.zeros(dst.shape, BF)

    zrow, zcol = iota((PACK, LANES), 0), iota((PACK, LANES), 1)
    ones = jnp.ones((amount, LANES), BF)
    dn = (((0,), (0,)), ((), ()))

    def local_states(z, get_k, get_v):
        total = jnp.zeros((HEAD_DIM, LANES), F32)
        pieces = []
        for i in range(n_pack):
            k, v = get_k(i), get_v(i)
            st = lax.dot_general(k, v, dn, preferred_element_type=F32)
            pieces.append(jnp.sum(jnp.where(same, st, 0.0).reshape(8, HEAD_DIM, PACK), axis=0))
            tot = lax.dot_general(k, ones, dn, preferred_element_type=F32)
            tot = jnp.where(zcol == 8 * i + zrow // HEAD_DIM, tot, 0.0)
            total = total + jnp.sum(tot.reshape(8, HEAD_DIM, LANES), axis=0)
        flat = jnp.concatenate(pieces + [total], axis=1)
        step = HEAD_DIM // n_cols
        for q in range(n_cols):
            part[z, q] = flat[q * step : (q + 1) * step]

    def rs_copy(z, k):
        peer = lax.rem(mc + k, n_cols)
        return pltpu.make_async_remote_copy(
            src_ref=part.at[z, peer], dst_ref=rs.at[z, k - 1],
            send_sem=red_send.at[z, 0, k - 1], recv_sem=red_recv.at[z, 0, k - 1],
            device_id=at(mr, peer), device_id_type=MESH,
        )

    def ar_copy(z, k):
        return pltpu.make_async_remote_copy(
            src_ref=ar_src.at[z], dst_ref=ar.at[z, k - 1],
            send_sem=red_send.at[z, 1, k - 1], recv_sem=red_recv.at[z, 1, k - 1],
            device_id=at(lax.rem(mr + k, n_rows), mc), device_id_type=MESH,
        )

    def ag_copy(z, k):
        return pltpu.make_async_remote_copy(
            src_ref=ag.at[z, mc], dst_ref=ag.at[z, mc],
            send_sem=red_send.at[z, 2, k - 1], recv_sem=red_recv.at[z, 2, k - 1],
            device_id=at(mr, lax.rem(mc + k, n_cols)), device_id_type=MESH,
        )

    def ag_wait(z, k):
        sender = lax.rem(mc - k + n_cols, n_cols)
        pltpu.make_async_remote_copy(
            src_ref=ag.at[z, mc], dst_ref=ag.at[z, sender],
            send_sem=red_send.at[z, 2, k - 1], recv_sem=red_recv.at[z, 2, k - 1],
            device_id=at(mr, sender), device_id_type=MESH,
        ).wait_recv()

    def reduce_1(z):
        for k in range(1, n_cols):
            rs_copy(z, k).start()

    def reduce_2(z):
        total = part[z, mc]
        for k in range(1, n_cols):
            rs_copy(z, k).wait_recv()
            total = total + rs[z, k - 1]
        ar_src[z] = total
        for k in range(1, n_rows):
            ar_copy(z, k).start()

    def reduce_3(z):
        total = ar_src[z]
        for k in range(1, n_rows):
            ar_copy(z, k).wait_recv()
            total = total + ar[z, k - 1]
        ag[z, mc] = total
        for k in range(1, n_cols):
            ag_copy(z, k).start()

    def reduce_4(z):
        for k in range(1, n_cols):
            ag_wait(z, k)
        return jnp.concatenate([ag[z, q] for q in range(n_cols)], axis=0)

    def conv(first, last):
        def chunk(ch, _):
            lanes = pl.ds(pl.multiple_of(ch * LANES, LANES), LANES)
            w = [taps[t, :, lanes] for t in range(25)]

            def line(r, _):
                sums = [None] * inner
                for a in range(5):
                    xs = [trip[r + a, jj, :, lanes] for jj in range(wide)]
                    for j in range(inner):
                        term = xs[j] * w[5 * a]
                        for b in range(1, 5):
                            term = term + xs[j + b] * w[5 * a + b]
                        sums[j] = term if a == 0 else sums[j] + term
                for j in range(inner):
                    spread[r, j, :, lanes] = sums[j]
                return 0

            lax.fori_loop(0, height, line, 0, unroll=2)
            return 0

        lax.fori_loop(first, last, chunk, 0)

    def native(t, i):
        lo = t * d + i * PACK
        return trip[2 : 2 + height, 2 : 2 + inner, :, lo : lo + PACK].reshape(amount, PACK)

    def grouped(t, i):
        lo = t * d + i * PACK
        return dot(spread[:, :, :, lo : lo + PACK].reshape(amount, PACK), gbd[t * n_pack + i]).astype(BF)

    def attend(z, flat, get_q):
        for i in range(n_pack):
            st = flat[:, i * PACK : (i + 1) * PACK]
            st = jnp.where(same, jnp.concatenate([st] * 8, axis=0), 0.0).astype(BF)
            head = one_hot(iota((LANES, PACK), 0) == 8 * i + iota((LANES, PACK), 1) // HEAD_DIM)
            tot = dot(flat[:, n_pack * PACK :].astype(BF), head)
            tot = jnp.where(same, jnp.concatenate([tot] * 8, axis=0), 0.0).astype(BF)
            q = feature_map(get_q(i).astype(F32)).astype(BF)
            att = (dot(q, st) / dot(q, tot)).astype(BF)
            add = dot(att, pw_ref[z * d + i * PACK : z * d + (i + 1) * PACK, :])
            if z == 0 and i == 0:
                acc[...] = add
            else:
                acc[...] += add

    local_states(0, lambda i: feature_map(native(1, i).astype(F32)).astype(BF), lambda i: native(2, i))
    reduce_1(0)
    for i in range(n_pack):
        tp = dot(dk_ref[:, third * i : third * (i + 1)].astype(BF), perm)
        for t in range(3):
            lo = t * d + i * PACK
            for tap in range(25):
                taps[tap, :, lo : lo + PACK] = jnp.broadcast_to(
                    tp[tap : tap + 1, t * PACK : (t + 1) * PACK], (SUB, PACK)
                ).astype(BF)
    n_group = gk_ref.shape[2]
    gk = gk_ref[...].reshape(HEAD_DIM * HEAD_DIM, n_group)
    grow, gcol = iota((n_group, PACK), 0), iota((n_group, PACK), 1)
    keep = iota((HEAD_DIM * HEAD_DIM, PACK), 0) % HEAD_DIM == iota((HEAD_DIM * HEAD_DIM, PACK), 1) % HEAD_DIM
    for t in range(3):
        for i in range(n_pack):
            g = dot(gk, one_hot(grow == 3 * (8 * i + gcol // HEAD_DIM) + t))
            g = jnp.sum(jnp.where(keep, g, 0.0).reshape(HEAD_DIM, HEAD_DIM, PACK), axis=1)
            gbd[t * n_pack + i] = jnp.where(same, jnp.concatenate([g] * 8, axis=0), 0.0).astype(BF)

    for i, way in enumerate(WAYS):
        @pl.when(exists((-way[0], -way[1])))
        def _():
            halo_copy(i).wait_recv()


    corners = halo_c[...].reshape(4 * SUB, d)
    size_k = base + 4 * SUB
    m, src = iota((size_m, size_k), 0), iota((size_m, size_k), 1)
    which = m // (wide * SUB)
    c = inner * (m % SUB) + (m // SUB) % wide - 2
    for p in range(2):
        lo = base + 2 * p * SUB + 2 * which
        want = jnp.where(c < 0, lo + c + 2, jnp.where(c >= breadth, lo + SUB + c - breadth, which * breadth + c))
        y = dot(one_hot(want == src), jnp.concatenate([halo_r[p].reshape(base, d), corners], axis=0)).astype(BF)
        first = p * (height + 2)
        trip[first : first + 2] = dot(y, wq[...]).astype(BF).reshape(2, wide, SUB, 3 * d)
    sides = dot(halo_e[...].reshape(2 * e, d), wq[...])
    spot = iota((SUB, 3 * d), 0)
    masks = (one_hot(spot == 0), one_hot(spot == SUB - 1))
    for r in range(height):
        for side in range(2):
            for b in range(2):
                at_row = side * e + 2 * r + b
                jj = side * (inner + 2) + b
                line = jnp.broadcast_to(sides[at_row : at_row + 1], (SUB, 3 * d)).astype(BF)
                trip[r + 2, jj] = trip[r + 2, jj] + line * masks[side]

    n_chunk = d // LANES
    conv(n_chunk, 2 * n_chunk)
    reduce_2(0)
    conv(2 * n_chunk, 3 * n_chunk)
    reduce_3(0)
    local_states(1, lambda i: feature_map(grouped(1, i).astype(F32)).astype(BF), lambda i: grouped(2, i))
    reduce_1(1)
    conv(0, n_chunk // 2)
    reduce_2(1)
    conv(n_chunk // 2, n_chunk)
    reduce_3(1)
    attend(0, reduce_4(0), lambda i: native(0, i))
    attend(1, reduce_4(1), lambda i: grouped(0, i))

    lines = 4
    size = lines * breadth
    m, src = iota((size, size), 0), iota((size, size), 1)
    cc = m % breadth
    back = one_hot(src == (m // breadth) * breadth + (cc % inner) * SUB + cc // inner)
    for b in range(height // lines):
        got = acc[b * size : (b + 1) * size, :] * gain_ref[...] + bias_ref[...]
        got = (got + res[b * lines : (b + 1) * lines].reshape(size, d).astype(F32)).astype(BF)
        out_ref[b * lines : (b + 1) * lines] = dot(back, got).astype(BF).reshape(lines, breadth, d)

    for i, way in enumerate(WAYS):
        @pl.when(exists(way))
        def _():
            halo_copy(i).wait_send()
    for z in range(2):
        for k in range(1, n_cols):
            rs_copy(z, k).wait_send()
            ag_copy(z, k).wait_send()
        for k in range(1, n_rows):
            ar_copy(z, k).wait_send()


def body(n_rows, n_cols, tokens, qkv_weight, depth_kernel, group_kernel, proj_weight, out_gain, out_bias):
    height, breadth, d = tokens.shape
    inner = breadth // SUB
    step = HEAD_DIM // n_cols
    msg = d + LANES
    most = max(n_rows, n_cols)
    vmem = pl.BlockSpec(memory_space=pltpu.VMEM)
    return pl.pallas_call(
        functools.partial(kernel, n_rows, n_cols),
        out_shape=jax.ShapeDtypeStruct((height, breadth, d), BF),
        in_specs=[vmem] * 7,
        out_specs=vmem,
        scratch_shapes=[
            pltpu.VMEM((2, 2 * height, d), BF),
            pltpu.VMEM((4, SUB, d), BF),
            pltpu.VMEM((2, 2 * height, d), BF),
            pltpu.VMEM((4, SUB, d), BF),
            pltpu.VMEM((2, 2, breadth, d), BF),
            pltpu.VMEM((d, 3 * d), BF),
            pltpu.VMEM((25, SUB, 3 * d), BF),
            pltpu.VMEM((3 * d // PACK, PACK, PACK), BF),
            pltpu.VMEM((height, inner, SUB, d), BF),
            pltpu.VMEM((height + 4, inner + 4, SUB, 3 * d), BF),
            pltpu.VMEM((height, inner, SUB, 3 * d), BF),
            pltpu.VMEM((height * breadth, d), F32),
            pltpu.VMEM((2, n_cols, step, msg), F32),
            pltpu.VMEM((2, n_cols - 1, step, msg), F32),
            pltpu.VMEM((2, step, msg), F32),
            pltpu.VMEM((2, n_rows - 1, step, msg), F32),
            pltpu.VMEM((2, n_cols, step, msg), F32),
            pltpu.SemaphoreType.DMA((8,)),
            pltpu.SemaphoreType.DMA((8,)),
            pltpu.SemaphoreType.DMA((2, 3, most)),
            pltpu.SemaphoreType.DMA((2, 3, most)),
        ],
        compiler_params=pltpu.CompilerParams(
            collective_id=0, has_side_effects=True, vmem_limit_bytes=56 * 1024 * 1024
        ),
        name="attention_module",
    )(tokens, qkv_weight, depth_kernel, jnp.transpose(group_kernel, (1, 2, 0)), proj_weight, out_gain[None, :], out_bias[None, :])


def solution(mesh):
    placed = (P(("groups", "rows"), "cols", None), P(), P(), P(), P(), P(), P())
    return jax.shard_map(
        functools.partial(body, mesh.shape["rows"], mesh.shape["cols"]),
        mesh=mesh,
        in_specs=placed,
        out_specs=P(("groups", "rows"), "cols", None),
        check_vma=False,
    )
```
